32 devices in a mesh: dp: 4 (over z), seq: 4 (over x, core), head: 2 (over y).
Axes of the slice: x: 2, y: 2, z: 4, core: 2. Of those that a mesh axis runs over, the one named last changes fastest.
Arguments:
- layer_in: bfloat16 [4, 1024, 768], P('dp', 'seq'), may hold values from -6 to 6
- cotangent: bfloat16 [4, 1024, 768], P('dp', 'seq'), may hold values from -6 to 6
- w_query: bfloat16 [768, 768], P('dp', 'head'), may hold values from -0.3125 to 0.3125
- w_key: bfloat16 [768, 768], P('dp', 'head'), may hold values from -0.21875 to 0.21875
- w_value: bfloat16 [768, 768], P('dp', 'head'), may hold values from -0.21875 to 0.21875
- w_out: bfloat16 [768, 768], P('dp', 'head'), may hold values from -0.875 to 0.875
- w_up: bfloat16 [768, 3072], P('dp', 'head'), may hold values from -0.21875 to 0.21875
- w_down: bfloat16 [768, 3072], P('dp', 'head'), may hold values from -0.109375 to 0.109375
- query_bias: float32 [768], P('head'), may hold values from -3 to 3
- value_bias: float32 [768], P('head'), may hold values from -3 to 3
- out_bias: float32 [768], replicated, may hold values from -3 to 3
- up_bias: float32 [3072], P('head'), may hold values from -3 to 3
- down_bias: float32 [768], replicated, may hold values from -3 to 3
- attn_gain: float32 [768], replicated, may hold values from 0.5 to 1.5
- attn_shift: float32 [768], replicated, may hold values from -2 to 2
- mlp_gain: float32 [768], replicated, may hold values from 0.5 to 1.5
- mlp_shift: float32 [768], replicated, may hold values from -2 to 2
Outputs:
- layer_out: bfloat16 [4, 1024, 768], P('dp', 'seq')
- grad_in: float32 [4, 1024, 768], P('dp', 'seq')
- grad_w_query: float32 [768, 768], P('dp', 'head')
- grad_w_key: float32 [768, 768], P('dp', 'head')
- grad_w_value: float32 [768, 768], P('dp', 'head')
- grad_w_out: float32 [768, 768], P('dp', 'head')
- grad_w_up: float32 [768, 3072], P('dp', 'head')
- grad_w_down: float32 [768, 3072], P('dp', 'head')
- grad_query_bias: float32 [768], P('head')
- grad_value_bias: float32 [768], P('head')
- grad_out_bias: float32 [768], replicated
- grad_up_bias: float32 [3072], P('head')
- grad_down_bias: float32 [768], replicated
- grad_attn_gain: float32 [768], replicated
- grad_attn_shift: float32 [768], replicated
- grad_mlp_gain: float32 [768], replicated
- grad_mlp_shift: float32 [768], replicated
The draws below stay inside these ranges and needn't reach their ends.
All inputs are finite; a program needn't handle non-finite values.
Results may differ from the reference program's by a relative error of at most 0.02.
Values may be sent and summed in bfloat16 or wider, within the bound.
No kernel may reach another device: no remote copies, remote signals or barrier semaphores. Data moves between devices by JAX's collectives and lax.ppermute only.
A program may use at most 64 MiB of HBM per device.

```python
import jax
import jax.numpy as jnp
from jax import lax

D = 768
HEADS = 12
HD = 64
FF = 3072
FRAMES = 1024
CLIPS = 4


def level_of(own_key, extent, cuts, smallest, top_value):
    level = 1.0
    for axis_at, parts in cuts:
        draws = jax.random.uniform(jax.random.fold_in(jax.random.fold_in(own_key, 6), axis_at), (parts,), jnp.float32, smallest / len(cuts), top_value / len(cuts))
        level = level * jnp.repeat(jnp.exp(draws), extent[axis_at] // parts).reshape((-1,) + (1,) * (len(extent) - 1 - axis_at))
    return level


def scatter_about(own_key, shape, scale, bound, shards=(), dtype=jnp.bfloat16):
    array = scale * jax.random.normal(own_key, shape, jnp.float32)
    if shards:
        array = array * level_of(own_key, shape, shards, -0.22, 0.18)
    return jnp.clip(array, -bound, bound).astype(dtype)


def setup_inputs(seed: int = 0) -> dict:
    key_of = jax.random.split(jax.random.key(seed), 18)
    return {
        "layer_in": scatter_about(key_of[0], (CLIPS, FRAMES, D), 1.0, 6.0, ((0, 4), (1, 4))),
        "cotangent": scatter_about(key_of[1], (CLIPS, FRAMES, D), 1.0, 6.0, ((0, 4), (1, 4))),
        "w_query": scatter_about(key_of[2], (D, D), (D // 2) ** -0.5, 0.3125, ((0, 4), (1, 2))),
        "w_key": scatter_about(key_of[3], (D, D), D ** -0.5, 0.21875, ((0, 4), (1, 2))),
        "w_value": scatter_about(key_of[4], (D, D), D ** -0.5, 0.21875, ((0, 4), (1, 2))),
        "w_out": scatter_about(key_of[5], (D, D), (D // 16) ** -0.5, 0.875, ((0, 4), (1, 2))),
        "w_up": scatter_about(key_of[6], (D, FF), D ** -0.5, 0.21875, ((0, 4), (1, 2))),
        "w_down": scatter_about(key_of[7], (D, FF), FF ** -0.5, 0.109375, ((0, 4), (1, 2))),
        "query_bias": scatter_about(key_of[8], (D,), 0.5, 3.0, ((0, 2),), jnp.float32),
        "value_bias": scatter_about(key_of[9], (D,), 0.5, 3.0, ((0, 2),), jnp.float32),
        "out_bias": scatter_about(key_of[10], (D,), 0.5, 3.0, (), jnp.float32),
        "up_bias": scatter_about(key_of[11], (FF,), 0.5, 3.0, ((0, 2),), jnp.float32),
        "down_bias": scatter_about(key_of[12], (D,), 0.5, 3.0, (), jnp.float32),
        "attn_gain": jnp.clip(1.0 + 0.1 * jax.random.normal(key_of[13], (D,), jnp.float32), 0.5, 1.5),
        "attn_shift": scatter_about(key_of[14], (D,), 0.3, 2.0, (), jnp.float32),
        "mlp_gain": jnp.clip(1.0 + 0.1 * jax.random.normal(key_of[15], (D,), jnp.float32), 0.5, 1.5),
        "mlp_shift": scatter_about(key_of[16], (D,), 0.3, 2.0, (), jnp.float32),
    }


NORM_EPS = 1e-05
SQRT_HALF = 0.7071067811865476
INV_ROOT_TWO_PI = 0.3989422804014327

def norm_forward(values, gain_vec, offset):
    mean_val = lax.optimization_barrier(jnp.mean(values, axis=-1, keepdims=True))
    centred = values - mean_val
    inverse = lax.rsqrt(lax.optimization_barrier(jnp.mean(centred * centred, axis=-1, keepdims=True)) + NORM_EPS)
    normed = centred * inverse
    return (normed, inverse, normed * gain_vec + offset)

def norm_backward(grad_rows, normed, inverse, gain_vec):
    scaled = grad_rows * gain_vec
    back_grad = inverse * (scaled - lax.optimization_barrier(jnp.mean(scaled, axis=-1, keepdims=True)) - normed * lax.optimization_barrier(jnp.mean(scaled * normed, axis=-1, keepdims=True)))
    return (back_grad, lax.optimization_barrier(jnp.sum(grad_rows * normed, axis=0)), lax.optimization_barrier(jnp.sum(grad_rows, axis=0)))

def gelu_value(pre_act):
    return 0.5 * pre_act * (1.0 + jax.scipy.special.erf(pre_act * SQRT_HALF))

def gelu_slope(pre_act):
    return 0.5 * (1.0 + jax.scipy.special.erf(pre_act * SQRT_HALF)) + pre_act * INV_ROOT_TWO_PI * jnp.exp(-0.5 * pre_act * pre_act)

def matmul(first_mat, second_mat):
    return jnp.dot(first_mat, second_mat, preferred_element_type=jnp.float32)

def rounded(values):
    return lax.optimization_barrier(values.astype(jnp.bfloat16)).astype(jnp.float32)

def one_clip(params, clip_in, grad_rows):
    w_query, w_key, w_value, w_out, w_up, w_down, query_bias, value_bias, out_bias, up_bias, down_bias, attn_gain, attn_shift, mlp_gain, mlp_shift = params
    frames = clip_in.shape[0]
    inputs = clip_in.astype(jnp.float32)
    attn_normed, attn_inverse, attn_affine = norm_forward(inputs, attn_gain, attn_shift)
    attn_act = attn_affine.astype(jnp.bfloat16)
    query_h = rounded(matmul(attn_act, w_query) + query_bias).reshape(frames, HEADS, HD)
    key_h = rounded(matmul(attn_act, w_key)).reshape(frames, HEADS, HD)
    value_h = rounded(matmul(attn_act, w_value) + value_bias).reshape(frames, HEADS, HD)
    scores = 0.125 * jnp.einsum('qhe,khe->hqk', query_h, key_h)
    row_max = lax.optimization_barrier(jnp.max(scores, axis=-1, keepdims=True))
    exp_scores = jnp.exp(scores - row_max)
    row_sum = lax.optimization_barrier(jnp.sum(exp_scores, axis=-1, keepdims=True))
    log_total = row_max + jnp.log(row_sum)
    weighted = jnp.einsum('hqk,khe->hqe', rounded(exp_scores), value_h) / row_sum
    context = jnp.transpose(weighted, (1, 0, 2)).reshape(frames, D).astype(jnp.bfloat16)
    context_h = lax.optimization_barrier(context).astype(jnp.float32).reshape(frames, HEADS, HD)
    resid_mid = inputs + matmul(context, w_out.T) + out_bias
    mlp_normed, mlp_inverse, mlp_affine = norm_forward(resid_mid, mlp_gain, mlp_shift)
    mlp_act = mlp_affine.astype(jnp.bfloat16)
    pre_act = matmul(mlp_act, w_up) + up_bias
    hidden = gelu_value(pre_act).astype(jnp.bfloat16)
    layer_out = (resid_mid + matmul(hidden, w_down.T) + down_bias).astype(jnp.bfloat16)
    grad_float = grad_rows.astype(jnp.float32)
    grad_down_bias = lax.optimization_barrier(jnp.sum(grad_float, axis=0))
    grad_w_down = matmul(grad_rows.T, hidden)
    d_pre = (matmul(grad_rows, w_down) * gelu_slope(pre_act)).astype(jnp.bfloat16)
    grad_up_bias = lax.optimization_barrier(jnp.sum(d_pre.astype(jnp.float32), axis=0))
    grad_w_up = matmul(mlp_act.T, d_pre)
    d_mlp_act = matmul(d_pre, w_up.T)
    mlp_back, grad_mlp_gain, grad_mlp_shift = norm_backward(d_mlp_act, mlp_normed, mlp_inverse, mlp_gain)
    d_mid = grad_float + mlp_back
    grad_out_bias = lax.optimization_barrier(jnp.sum(d_mid, axis=0))
    d_mid_round = d_mid.astype(jnp.bfloat16)
    grad_w_out = matmul(d_mid_round.T, context)
    dctx_h = rounded(matmul(d_mid_round, w_out)).reshape(frames, HEADS, HD)
    delta_row = jnp.transpose(lax.optimization_barrier(jnp.sum(dctx_h * context_h, axis=-1)))
    prob_mat = jnp.exp(scores - log_total)
    d_prob = jnp.einsum('qhe,khe->hqk', dctx_h, value_h)
    d_score = rounded(0.125 * prob_mat * (d_prob - delta_row[:, :, None]))
    d_query = jnp.einsum('hqk,khe->qhe', d_score, key_h).reshape(frames, D)
    d_key = jnp.einsum('hqk,qhe->khe', d_score, query_h).reshape(frames, D)
    d_value = jnp.einsum('hqk,qhe->khe', rounded(prob_mat), dctx_h).reshape(frames, D)
    grad_query_bias = lax.optimization_barrier(jnp.sum(d_query, axis=0))
    grad_value_bias = lax.optimization_barrier(jnp.sum(d_value, axis=0))
    query_round = d_query.astype(jnp.bfloat16)
    key_round = d_key.astype(jnp.bfloat16)
    value_round = d_value.astype(jnp.bfloat16)
    grad_w_query = matmul(attn_act.T, query_round)
    grad_w_key = matmul(attn_act.T, key_round)
    grad_w_value = matmul(attn_act.T, value_round)
    d_attn_act = matmul(query_round, w_query.T) + matmul(key_round, w_key.T) + matmul(value_round, w_value.T)
    attn_back, grad_attn_gain, grad_attn_shift = norm_backward(d_attn_act, attn_normed, attn_inverse, attn_gain)
    grad_in = d_mid + attn_back
    grads = (grad_w_query, grad_w_key, grad_w_value, grad_w_out, grad_w_up, grad_w_down, grad_query_bias, grad_value_bias, grad_out_bias, grad_up_bias, grad_down_bias, grad_attn_gain, grad_attn_shift, grad_mlp_gain, grad_mlp_shift)
    return (layer_out, grad_in, grads)

def reference(layer_in, cotangent, w_query, w_key, w_value, w_out, w_up, w_down, query_bias, value_bias, out_bias, up_bias, down_bias, attn_gain, attn_shift, mlp_gain, mlp_shift):
    params = (w_query, w_key, w_value, w_out, w_up, w_down, query_bias, value_bias, out_bias, up_bias, down_bias, attn_gain, attn_shift, mlp_gain, mlp_shift)
    start_sums = (jnp.zeros((D, D), jnp.float32), jnp.zeros((D, D), jnp.float32), jnp.zeros((D, D), jnp.float32), jnp.zeros((D, D), jnp.float32), jnp.zeros((D, FF), jnp.float32), jnp.zeros((D, FF), jnp.float32), jnp.zeros((D,), jnp.float32), jnp.zeros((D,), jnp.float32), jnp.zeros((D,), jnp.float32), jnp.zeros((FF,), jnp.float32), jnp.zeros((D,), jnp.float32), jnp.zeros((D,), jnp.float32), jnp.zeros((D,), jnp.float32), jnp.zeros((D,), jnp.float32), jnp.zeros((D,), jnp.float32))

    def scan_step(grad_sums, clip_pair):
        clip_in, grad_rows = clip_pair
        layer_out, grad_in, grads = one_clip(params, clip_in, grad_rows)
        return (jax.tree.map(jnp.add, grad_sums, grads), (layer_out, grad_in))
    grad_sums, outputs = lax.scan(scan_step, start_sums, (layer_in, cotangent))
    return (outputs[0], outputs[1], grad_sums[0], grad_sums[1], grad_sums[2], grad_sums[3], grad_sums[4], grad_sums[5], grad_sums[6], grad_sums[7], grad_sums[8], grad_sums[9], grad_sums[10], grad_sums[11], grad_sums[12], grad_sums[13], grad_sums[14])
```

```python
import jax
import jax.numpy as jnp
from jax import lax
from jax.sharding import PartitionSpec as P

HD = 64
NORM_EPS = 1e-05
SQRT_HALF = 0.7071067811865476
INV_ROOT_TWO_PI = 0.3989422804014327
BF = jnp.bfloat16
F32 = jnp.float32


def mm(a, b):
    return jnp.dot(a, b, preferred_element_type=F32)


def mm_nt(a, b):
    return lax.dot_general(a, b, (((1,), (1,)), ((), ())), preferred_element_type=F32)


def mm_tn(a, b):
    return lax.dot_general(a, b, (((0,), (0,)), ((), ())), preferred_element_type=F32)


def norm_parts(values):
    mean_val = jnp.mean(values, axis=-1, keepdims=True)
    centred = values - mean_val
    inverse = lax.rsqrt(jnp.mean(centred * centred, axis=-1, keepdims=True) + NORM_EPS)
    return centred * inverse, inverse


def norm_backward(grad_rows, normed, inverse, gain_vec):
    scaled = grad_rows * gain_vec
    return inverse * (
        scaled
        - jnp.mean(scaled, axis=-1, keepdims=True)
        - normed * jnp.mean(scaled * normed, axis=-1, keepdims=True)
    )


def after(value, *others):
    return lax.optimization_barrier((value, *others))[0]


def make_moves(mesh):
    n_dp, n_seq, n_head = mesh.shape["dp"], mesh.shape["seq"], mesh.shape["head"]

    def core(v):
        return lax.ppermute(v, "seq", [(i, i ^ 1) for i in range(n_seq)])

    def across(v):
        return lax.ppermute(v, "seq", [(i, i ^ 2) for i in range(n_seq)])

    def beside(v):
        return lax.ppermute(v, "head", [(i, i ^ 1) for i in range(n_head)])

    def corner(v):
        pairs = [
            (s * n_head + h, (s ^ 2) * n_head + (h ^ 1))
            for s in range(n_seq)
            for h in range(n_head)
        ]
        return lax.ppermute(v, ("seq", "head"), pairs)

    def along(v, k):
        return lax.ppermute(v, "dp", [(i, i ^ k) for i in range(n_dp)])

    return n_dp, core, across, beside, corner, along


def per_device(
    mesh,
    layer_in,
    cotangent,
    w_query,
    w_key,
    w_value,
    w_out,
    w_up,
    w_down,
    query_bias,
    value_bias,
    out_bias,
    up_bias,
    down_bias,
    attn_gain,
    attn_shift,
    mlp_gain,
    mlp_shift,
):
    n_dp, core, across, beside, corner, along = make_moves(mesh)
    own_z = lax.axis_index("dp")
    own_s = lax.axis_index("seq")
    own_y = lax.axis_index("head")
    own_x, own_c = own_s // 2, own_s % 2
    fr, width = layer_in.shape[1], layer_in.shape[2]
    quarter = fr // 2
    rows = width // n_dp
    half = rows // 2
    aw = w_query.shape[1] // 2
    fw = w_up.shape[1] // 2
    heads = aw // HD

    def rolled(a):
        return jnp.concatenate(
            [
                lax.dynamic_slice_in_dim(a, own_y * quarter, quarter, 0),
                lax.dynamic_slice_in_dim(a, (1 - own_y) * quarter, quarter, 0),
            ],
            axis=0,
        )

    def weight_cut(w, cols):
        return lax.dynamic_slice(w, (own_c * half, own_x * cols), (half, cols))

    def gathered(piece):
        pieces = [(own_z, piece)] + [(own_z ^ k, along(piece, k)) for k in range(1, n_dp)]
        buf = jnp.zeros((n_dp,) + piece.shape, piece.dtype)
        for at, part in pieces:
            buf = lax.dynamic_update_slice(buf, part[None], (at, 0, 0))
        return buf, pieces[-1][1]

    def merged(buf):
        other = core(buf)
        first = jnp.where(own_c == 0, buf, other)
        second = jnp.where(own_c == 0, other, buf)
        return jnp.stack([first, second], axis=1).reshape(width, buf.shape[2])

    attn_piece = jnp.concatenate(
        [weight_cut(w, aw) for w in (w_query, w_key, w_value, w_out)], axis=1
    )
    attn_buf, attn_last = gathered(attn_piece)
    mine = rolled(layer_in[0])
    rows_in = jnp.concatenate([mine, across(mine)], axis=0)
    inputs = rows_in.astype(F32)
    attn_normed, attn_inverse = norm_parts(inputs)
    attn_act = (attn_normed * attn_gain + attn_shift).astype(BF)
    act_all = jnp.concatenate([attn_act, core(attn_act)], axis=0)
    attn_full = merged(attn_buf)
    wq, wk, wv, wo = (attn_full[:, i * aw : (i + 1) * aw] for i in range(4))

    ff_piece = jnp.concatenate([weight_cut(w, fw) for w in (w_up, w_down)], axis=1)
    ff_piece = after(ff_piece, attn_last)
    ff_buf, _ = gathered(ff_piece)
    cot_mine = after(rolled(cotangent[0]), attn_last)
    cot = jnp.concatenate([cot_mine, across(cot_mine)], axis=0)

    q_bias = lax.dynamic_slice_in_dim(query_bias, own_x * aw, aw, 0)
    v_bias = lax.dynamic_slice_in_dim(value_bias, own_x * aw, aw, 0)
    u_bias = lax.dynamic_slice_in_dim(up_bias, own_x * fw, fw, 0)

    query = (mm(attn_act, wq) + q_bias).astype(BF)
    keys = mm(act_all, wk).astype(BF)
    values = (mm(act_all, wv) + v_bias).astype(BF)

    def head_of(a, h):
        return a[:, h * HD : (h + 1) * HD]

    context, log_total = [], []
    for h in range(heads):
        scores = 0.125 * mm_nt(head_of(query, h), head_of(keys, h))
        row_max = jnp.max(scores, axis=-1, keepdims=True)
        exp_scores = jnp.exp(scores - row_max)
        row_sum = jnp.sum(exp_scores, axis=-1, keepdims=True)
        log_total.append(row_max + jnp.log(row_sum))
        context.append((mm(exp_scores.astype(BF), head_of(values, h)) / row_sum).astype(BF))
    context = jnp.concatenate(context, axis=1)

    def part(a, i):
        return a[i * quarter : (i + 1) * quarter]

    def reduced(partial):
        got = [
            move(part(partial, i).astype(BF))
            for i, move in ((1, beside), (2, across), (3, corner))
        ]
        total = part(partial, 0)
        for g in got:
            total = total + g.astype(F32)
        return total

    def spread(own):
        return jnp.concatenate([own, beside(own), across(own), corner(own)], axis=0)

    def both(own):
        other = beside(own)
        return jnp.where(
            own_y == 0,
            jnp.concatenate([own, other], axis=0),
            jnp.concatenate([other, own], axis=0),
        )

    attn_out = reduced(mm_nt(context, wo))
    resid_mid = part(inputs, 0) + attn_out + out_bias
    mlp_normed, mlp_inverse = norm_parts(resid_mid)
    mlp_own = (mlp_normed * mlp_gain + mlp_shift).astype(BF)
    mlp_act = spread(mlp_own)

    ff_full = merged(ff_buf)
    wu, wd = ff_full[:, :fw], ff_full[:, fw:]
    pre_act = mm(mlp_act, wu) + u_bias
    cdf = 0.5 * (1.0 + jax.scipy.special.erf(pre_act * SQRT_HALF))
    hidden = (pre_act * cdf).astype(BF)
    slope = cdf + pre_act * INV_ROOT_TWO_PI * jnp.exp(-0.5 * pre_act * pre_act)
    d_pre = (mm(cot, wd) * slope).astype(BF)
    d_mlp_act = reduced(mm_nt(d_pre, wu))

    cot_own = part(cot, 0).astype(F32)
    d_mid = cot_own + norm_backward(d_mlp_act, mlp_normed, mlp_inverse, mlp_gain)
    d_mid_all = spread(d_mid.astype(BF))

    layer_out = both((resid_mid + reduced(mm_nt(hidden, wd)) + down_bias).astype(BF))

    def shard_sums(grad):
        cols = grad.shape[1]
        cut = grad.reshape(n_dp, 2, half, cols)
        keep = lax.dynamic_index_in_dim(cut, own_c, 1, keepdims=False)
        give = lax.dynamic_index_in_dim(cut, 1 - own_c, 1, keepdims=False).astype(BF)
        keep = keep + core(give).astype(F32)
        total = lax.dynamic_index_in_dim(keep, own_z, 0, keepdims=False)
        sent = [
            along(lax.dynamic_index_in_dim(keep, own_z ^ k, 0, keepdims=False).astype(BF), k)
            for k in range(1, n_dp)
        ]
        for got in sent:
            total = total + got.astype(F32)
        total = total.astype(BF)
        other = across(total)
        wide = jnp.stack(
            [jnp.where(own_x == 0, total, other), jnp.where(own_x == 0, other, total)], axis=0
        )
        other = core(wide)
        tall = jnp.concatenate(
            [jnp.where(own_c == 0, wide, other), jnp.where(own_c == 0, other, wide)], axis=1
        )
        return tall

    def shard_of(tall, at, cols):
        return jnp.concatenate(
            [tall[0, :, at : at + cols], tall[1, :, at : at + cols]], axis=1
        ).astype(F32)

    ff_shards = shard_sums(jnp.concatenate([mm_tn(mlp_act, d_pre), mm_tn(cot, hidden)], axis=1))
    grad_w_up, grad_w_down = shard_of(ff_shards, 0, fw), shard_of(ff_shards, fw, fw)

    def placed(vec, size):
        return lax.dynamic_update_slice_in_dim(
            jnp.zeros((size,), F32), vec, own_x * vec.shape[0], 0
        )

    def vector_sums(head_parts, whole_parts):
        vec = jnp.concatenate([*head_parts, *whole_parts])
        split = sum(p.shape[0] for p in head_parts)
        k = 1
        while k < n_dp:
            vec = vec + along(vec, k)
            k *= 2
        vec = vec + across(vec)
        vec = vec + core(vec)
        tail = vec[split:]
        tail = tail + beside(tail)
        return vec[:split], tail

    def rowsum(a):
        return jnp.sum(a, axis=0)

    up_sum, early = vector_sums(
        [placed(rowsum(d_pre.astype(F32)), 2 * fw)],
        [
            rowsum(cot_own),
            rowsum(d_mlp_act * mlp_normed),
            rowsum(d_mlp_act),
            rowsum(d_mid),
        ],
    )

    d_context = mm(d_mid_all, wo).astype(BF)
    d_query, d_key, d_value = [], [], []
    for h in range(heads):
        qh, kh, vh = head_of(query, h), head_of(keys, h), head_of(values, h)
        dch, ch = head_of(d_context, h), head_of(context, h)
        delta = jnp.sum(dch.astype(F32) * ch.astype(F32), axis=-1, keepdims=True)
        prob = jnp.exp(0.125 * mm_nt(qh, kh) - log_total[h])
        d_score = (0.125 * prob * (mm_nt(dch, vh) - delta)).astype(BF)
        d_query.append(mm(d_score, kh))
        d_key.append(mm_tn(d_score, qh))
        d_value.append(mm_tn(prob.astype(BF), dch))
    d_query = jnp.concatenate(d_query, axis=1)
    d_kv = jnp.concatenate(d_key + d_value, axis=1)
    own_rows = 2 * fr
    d_kv = d_kv[:own_rows] + core(d_kv[own_rows:].astype(BF)).astype(F32)
    query_round = d_query.astype(BF)
    kv_round = d_kv.astype(BF)
    key_round, value_round = kv_round[:, :aw], kv_round[:, aw:]
    attn_terms = mm_nt(query_round, wq) + mm_nt(key_round, wk) + mm_nt(value_round, wv)
    d_attn_act = reduced(attn_terms)
    grad_in = d_mid + norm_backward(
        d_attn_act, part(attn_normed, 0), part(attn_inverse, 0), attn_gain
    )
    grad_in = both(grad_in.astype(BF)).astype(F32)

    head_sums, late = vector_sums(
        [placed(rowsum(d_query), 2 * aw), placed(rowsum(d_kv[:, aw:]), 2 * aw)],
        [rowsum(attn_terms * attn_normed), rowsum(attn_terms)],
    )
    attn_shards = shard_sums(
        jnp.concatenate(
            [
                mm_tn(attn_act, query_round),
                mm_tn(attn_act, key_round),
                mm_tn(attn_act, value_round),
                mm_tn(d_mid_all, context),
            ],
            axis=1,
        )
    )
    grad_w_query, grad_w_key, grad_w_value, grad_w_out = (
        shard_of(attn_shards, i * aw, aw) for i in range(4)
    )
    return (
        layer_out[None],
        grad_in[None],
        grad_w_query,
        grad_w_key,
        grad_w_value,
        grad_w_out,
        grad_w_up,
        grad_w_down,
        head_sums[: 2 * aw],
        head_sums[2 * aw :],
        early[3 * width :],
        up_sum,
        early[:width],
        late[:width],
        late[width:],
        early[width : 2 * width],
        early[2 * width : 3 * width],
    )


def solution(mesh):
    square = P("dp", "head")
    acts = P("dp", "seq", None)
    return jax.shard_map(
        lambda *args: per_device(mesh, *args),
        mesh=mesh,
        in_specs=(acts,) * 2
        + (square,) * 6
        + (P("head"), P("head"), P(), P("head"), P(), P(), P(), P(), P()),
        out_specs=(acts,) * 2
        + (square,) * 6
        + (P("head"), P("head"), P(), P("head"), P(), P(), P(), P(), P()),
        check_vma=False,
    )
```

```python
import jax
import jax.numpy as jnp
from jax import lax
from jax.experimental import pallas as pl
from jax.experimental.pallas import tpu as pltpu
from jax.sharding import PartitionSpec as P


HD = 64
NORM_EPS = 1e-05
SQRT_HALF = 0.7071067811865476
INV_ROOT_TWO_PI = 0.3989422804014327
BF = jnp.bfloat16
F32 = jnp.float32


def mm(a, b):
    return jnp.dot(a, b, preferred_element_type=F32)


def mm_nt(a, b):
    return lax.dot_general(a, b, (((1,), (1,)), ((), ())), preferred_element_type=F32)


def mm_tn(a, b):
    return lax.dot_general(a, b, (((0,), (0,)), ((), ())), preferred_element_type=F32)


def norm_parts(values):
    mean_val = jnp.mean(values, axis=-1, keepdims=True)
    centred = values - mean_val
    inverse = lax.rsqrt(jnp.mean(centred * centred, axis=-1, keepdims=True) + NORM_EPS)
    return centred * inverse, inverse


def norm_backward(grad_rows, normed, inverse, gain_vec):
    scaled = grad_rows * gain_vec
    return inverse * (
        scaled
        - jnp.mean(scaled, axis=-1, keepdims=True)
        - normed * jnp.mean(scaled * normed, axis=-1, keepdims=True)
    )


def after(value, *others):
    return lax.optimization_barrier((value, *others))[0]


MIB = 1024 * 1024
VM = pl.BlockSpec(memory_space=pltpu.VMEM)


def assemble(pieces):
    n, (rows, cols) = len(pieces), pieces[0].shape

    def kernel(*refs):
        own = lax.axis_index("dp")
        for k in range(n):
            at = pl.multiple_of(jnp.bitwise_xor(own, k) * rows, rows)
            refs[n][pl.ds(at, rows), :] = refs[k][...]

    return pl.pallas_call(
        kernel,
        out_shape=jax.ShapeDtypeStruct((n * rows, cols), pieces[0].dtype),
        in_specs=[VM] * n,
        out_specs=VM,
        cost_estimate=pl.CostEstimate(
            flops=0, transcendentals=0, bytes_accessed=4 * n * rows * cols
        ),
        compiler_params=pltpu.CompilerParams(vmem_limit_bytes=8 * MIB),
        name="assemble",
    )(*pieces)


def finish(wide, other, count):
    rows, cols = wide.shape[1], wide.shape[2] // count

    def kernel(mine_ref, other_ref, *outs):
        own_c = lax.rem(lax.axis_index("seq"), 2)

        def put(first, second):
            for m, src in enumerate((first, second)):
                for i in range(count):
                    for x in range(2):
                        outs[m * count + i][:, x * cols : (x + 1) * cols] = src[
                            x, :, i * cols : (i + 1) * cols
                        ].astype(F32)

        @pl.when(own_c == 0)
        def _():
            put(mine_ref, other_ref)

        @pl.when(own_c == 1)
        def _():
            put(other_ref, mine_ref)

    return pl.pallas_call(
        kernel,
        out_shape=[jax.ShapeDtypeStruct((rows, 2 * cols), F32)] * (2 * count),
        in_specs=[VM] * 2,
        out_specs=[VM] * (2 * count),
        cost_estimate=pl.CostEstimate(
            flops=0, transcendentals=0, bytes_accessed=24 * rows * cols * count
        ),
        compiler_params=pltpu.CompilerParams(vmem_limit_bytes=8 * MIB),
        name="finish",
    )(wide, other)


def attention_front(query, own_kv, other_kv, width):
    rows = query.shape[0]
    block = rows // 2

    def kernel(q_ref, own_ref, oth_ref, c_ref, lt_ref):
        c_ref[:, :width] = jnp.zeros((rows, width), BF)
        for h in range(width // HD):
            cols = slice(h * HD, (h + 1) * HD)
            late = slice(width + h * HD, width + (h + 1) * HD)
            for at in range(0, rows, block):
                qh = q_ref[at : at + block, cols]
                first = 0.125 * mm_nt(qh, own_ref[:, cols])
                second = 0.125 * mm_nt(qh, oth_ref[:, cols])
                row_max = jnp.maximum(
                    jnp.max(first, axis=-1, keepdims=True), jnp.max(second, axis=-1, keepdims=True)
                )
                first = jnp.exp(first - row_max)
                second = jnp.exp(second - row_max)
                row_sum = jnp.sum(first, axis=-1, keepdims=True) + jnp.sum(
                    second, axis=-1, keepdims=True
                )
                total = mm(first.astype(BF), own_ref[:, late]) + mm(
                    second.astype(BF), oth_ref[:, late]
                )
                c_ref[at : at + block, late] = (total / row_sum).astype(BF)
                lt_ref[at : at + block, h : h + 1] = row_max + jnp.log(row_sum)

    return pl.pallas_call(
        kernel,
        out_shape=[
            jax.ShapeDtypeStruct((rows, 2 * width), BF),
            jax.ShapeDtypeStruct((rows, 128), F32),
        ],
        in_specs=[VM] * 3,
        out_specs=[VM] * 2,
        cost_estimate=pl.CostEstimate(
            flops=8 * rows * rows * width,
            transcendentals=2 * rows * rows * (width // HD),
            bytes_accessed=12 * rows * width,
        ),
        compiler_params=pltpu.CompilerParams(vmem_limit_bytes=24 * MIB),
        name="attention_front",
    )(query, own_kv, other_kv)


def attention_back(query, own_kv, other_kv, context, d_context, log_total, width):
    rows = query.shape[0]

    def kernel(
        q_ref, own_ref, oth_ref, c_ref, dc_ref, lt_ref, dq_ref, down_ref, doth_ref, qs_ref, vs_ref
    ):
        dq_ref[:, width:] = jnp.zeros((rows, width), BF)
        for h in range(width // HD):
            cols = slice(h * HD, (h + 1) * HD)
            late = slice(width + h * HD, width + (h + 1) * HD)
            qh, ch, dch = q_ref[:, cols], c_ref[:, late], dc_ref[:, late]
            delta = jnp.sum(dch.astype(F32) * ch.astype(F32), axis=-1, keepdims=True)
            total = lt_ref[:, h : h + 1]
            d_query = jnp.zeros((rows, HD), F32)
            sums = jnp.zeros((1, HD), F32)
            for src, out in ((own_ref, down_ref), (oth_ref, doth_ref)):
                kh, vh = src[:, cols], src[:, late]
                prob = jnp.exp(0.125 * mm_nt(qh, kh) - total)
                d_score = (0.125 * prob * (mm_nt(dch, vh) - delta)).astype(BF)
                d_query = d_query + mm(d_score, kh)
                out[:, cols] = mm_tn(d_score, qh).astype(out.dtype)
                d_value = mm_tn(prob.astype(BF), dch)
                out[:, late] = d_value.astype(out.dtype)
                sums = sums + jnp.sum(d_value, axis=0, keepdims=True)
            dq_ref[:, cols] = d_query.astype(BF)
            qs_ref[:, cols] = jnp.sum(d_query, axis=0, keepdims=True)
            vs_ref[:, cols] = sums

    return pl.pallas_call(
        kernel,
        out_shape=[
            jax.ShapeDtypeStruct((rows, 2 * width), BF),
            jax.ShapeDtypeStruct((rows, 2 * width), F32),
            jax.ShapeDtypeStruct((rows, 2 * width), BF),
            jax.ShapeDtypeStruct((1, width), F32),
            jax.ShapeDtypeStruct((1, width), F32),
        ],
        in_specs=[VM] * 6,
        out_specs=[VM] * 5,
        cost_estimate=pl.CostEstimate(
            flops=20 * rows * rows * width,
            transcendentals=2 * rows * rows * (width // HD),
            bytes_accessed=20 * rows * width,
        ),
        compiler_params=pltpu.CompilerParams(vmem_limit_bytes=24 * MIB),
        name="attention_back",
    )(query, own_kv, other_kv, context, d_context, log_total)


def quarters(pairs, normed=None):
    rows, width = pairs[0][0].shape[0], pairs[0][1].shape[0]
    quarter = rows // 4
    n = len(pairs)
    extra = [] if normed is None else [normed]

    def kernel(*refs):
        outs = refs[2 * n + len(extra) :]
        for i in range(4):
            at = slice(i * quarter, (i + 1) * quarter)
            total = mm_nt(refs[0][at, :], refs[1][...])
            for p in range(1, n):
                total = total + mm_nt(refs[2 * p][at, :], refs[2 * p + 1][...])
            outs[i][...] = total.astype(outs[i].dtype)
            if extra:
                gain_sum = jnp.sum(total * refs[2 * n][at, :], axis=0, keepdims=True)
                shift_sum = jnp.sum(total, axis=0, keepdims=True)
                if i == 0:
                    outs[4][...] = gain_sum
                    outs[5][...] = shift_sum
                else:
                    outs[4][...] += gain_sum
                    outs[5][...] += shift_sum

    return pl.pallas_call(
        kernel,
        out_shape=[jax.ShapeDtypeStruct((quarter, width), F32)]
        + [jax.ShapeDtypeStruct((quarter, width), BF)] * 3
        + [jax.ShapeDtypeStruct((1, width), F32)] * (2 * len(extra)),
        in_specs=[VM] * (2 * n + len(extra)),
        out_specs=[VM] * (4 + 2 * len(extra)),
        cost_estimate=pl.CostEstimate(
            flops=2 * n * rows * width * pairs[0][0].shape[1],
            transcendentals=0,
            bytes_accessed=4 * rows * width,
        ),
        compiler_params=pltpu.CompilerParams(vmem_limit_bytes=16 * MIB),
        name="quarters",
    )(*[a for pair in pairs for a in pair], *extra)


def norm_middle(own, others, rows_in, bias, gain, shift):
    def kernel(own_ref, a_ref, b_ref, c_ref, in_ref, bias_ref, gain_ref, shift_ref, mid_ref, act_ref):
        total = own_ref[...] + a_ref[...].astype(F32)
        total = total + b_ref[...].astype(F32) + c_ref[...].astype(F32)
        mid = in_ref[...].astype(F32) + total + bias_ref[...]
        mid_ref[...] = mid
        act_ref[...] = (norm_parts(mid)[0] * gain_ref[...] + shift_ref[...]).astype(BF)

    return pl.pallas_call(
        kernel,
        out_shape=[jax.ShapeDtypeStruct(own.shape, F32), jax.ShapeDtypeStruct(own.shape, BF)],
        in_specs=[VM] * 8,
        out_specs=[VM] * 2,
        cost_estimate=pl.CostEstimate(
            flops=20 * own.size, transcendentals=0, bytes_accessed=18 * own.size
        ),
        compiler_params=pltpu.CompilerParams(vmem_limit_bytes=8 * MIB),
        name="norm_middle",
    )(own, *others, rows_in, bias[None], gain[None], shift[None])


def norm_middle_back(own, others, mid, cotangent, gain):
    def kernel(own_ref, a_ref, b_ref, c_ref, mid_ref, cot_ref, gain_ref, d_ref, dr_ref, sum_ref):
        grad = own_ref[...] + a_ref[...].astype(F32)
        grad = grad + b_ref[...].astype(F32) + c_ref[...].astype(F32)
        normed, inverse = norm_parts(mid_ref[...])
        cot = cot_ref[...].astype(F32)
        d_mid = cot + norm_backward(grad, normed, inverse, gain_ref[...])
        d_ref[...] = d_mid
        dr_ref[...] = d_mid.astype(BF)
        for i, rows in enumerate((d_mid, cot, grad * normed, grad)):
            sum_ref[i : i + 1, :] = jnp.sum(rows, axis=0, keepdims=True)

    return pl.pallas_call(
        kernel,
        out_shape=[
            jax.ShapeDtypeStruct(own.shape, F32),
            jax.ShapeDtypeStruct(own.shape, BF),
            jax.ShapeDtypeStruct((4, own.shape[1]), F32),
        ],
        in_specs=[VM] * 7,
        out_specs=[VM] * 3,
        cost_estimate=pl.CostEstimate(
            flops=30 * own.size, transcendentals=0, bytes_accessed=24 * own.size
        ),
        compiler_params=pltpu.CompilerParams(vmem_limit_bytes=8 * MIB),
        name="norm_middle_back",
    )(own, *others, mid, cotangent, gain[None])


def packed(q_sum, v_sum, up_sum, gain_sum, shift_sum, middle):
    width, aw = gain_sum.shape[1], q_sum.shape[1]

    def kernel(q_ref, v_ref, up_ref, gain_ref, shift_ref, mid_ref, out_ref):
        own_x = lax.axis_index("seq") // 2
        out_ref[...] = jnp.zeros((16, width), F32)
        for x in range(2):

            @pl.when(own_x == x)
            def _():
                out_ref[x : x + 1, :] = up_ref[...]
                out_ref[2:3, x * aw : (x + 1) * aw] = q_ref[...]
                out_ref[2:3, (2 + x) * aw : (3 + x) * aw] = v_ref[...]

        out_ref[8:12, :] = mid_ref[...]
        out_ref[12:13, :] = gain_ref[...]
        out_ref[13:14, :] = shift_ref[...]

    return pl.pallas_call(
        kernel,
        out_shape=jax.ShapeDtypeStruct((16, width), F32),
        in_specs=[VM] * 6,
        out_specs=VM,
        cost_estimate=pl.CostEstimate(flops=0, transcendentals=0, bytes_accessed=100 * width),
        compiler_params=pltpu.CompilerParams(vmem_limit_bytes=4 * MIB),
        name="packed",
    )(q_sum, v_sum, up_sum, gain_sum, shift_sum, middle)


def make_moves(mesh):
    n_dp, n_seq, n_head = mesh.shape["dp"], mesh.shape["seq"], mesh.shape["head"]

    def core(v):
        return lax.ppermute(v, "seq", [(i, i ^ 1) for i in range(n_seq)])

    def across(v):
        return lax.ppermute(v, "seq", [(i, i ^ 2) for i in range(n_seq)])

    def beside(v):
        return lax.ppermute(v, "head", [(i, i ^ 1) for i in range(n_head)])

    def corner(v):
        pairs = [
            (s * n_head + h, (s ^ 2) * n_head + (h ^ 1))
            for s in range(n_seq)
            for h in range(n_head)
        ]
        return lax.ppermute(v, ("seq", "head"), pairs)

    def along(v, k):
        return lax.ppermute(v, "dp", [(i, i ^ k) for i in range(n_dp)])

    return n_dp, core, across, beside, corner, along


def per_device(
    mesh,
    layer_in,
    cotangent,
    w_query,
    w_key,
    w_value,
    w_out,
    w_up,
    w_down,
    query_bias,
    value_bias,
    out_bias,
    up_bias,
    down_bias,
    attn_gain,
    attn_shift,
    mlp_gain,
    mlp_shift,
):
    n_dp, core, across, beside, corner, along = make_moves(mesh)
    own_z = lax.axis_index("dp")
    own_s = lax.axis_index("seq")
    own_y = lax.axis_index("head")
    own_x, own_c = own_s // 2, own_s % 2
    fr, width = layer_in.shape[1], layer_in.shape[2]
    quarter = fr // 2
    rows = width // n_dp
    aw = w_query.shape[1] // 2
    fw = w_up.shape[1] // 2

    def rolled(a):
        return jnp.concatenate(
            [
                lax.dynamic_slice_in_dim(a, own_y * quarter, quarter, 0),
                lax.dynamic_slice_in_dim(a, (1 - own_y) * quarter, quarter, 0),
            ],
            axis=0,
        )

    def chip_cut(w):
        cols = w.shape[1] // 2
        return jnp.where(own_x == 0, w[:, :cols], w[:, cols:])

    def by_core(first, second):
        return jnp.where(own_c == 0, first, second)

    def gathered(piece):
        pieces = [piece] + [along(piece, k) for k in range(1, n_dp)]
        if rows % 16 == 0:
            mine = assemble(pieces)
        else:
            buf = jnp.zeros((n_dp,) + piece.shape, piece.dtype)
            for k, part in enumerate(pieces):
                buf = lax.dynamic_update_slice(buf, part[None], (own_z ^ k, 0, 0))
            mine = buf.reshape(width, piece.shape[1])
        other = core(mine)
        return by_core(mine, other), by_core(other, mine), mine

    attn_piece = by_core(
        jnp.concatenate([chip_cut(w_key), chip_cut(w_value)], axis=1),
        jnp.concatenate([chip_cut(w_query), chip_cut(w_out)], axis=1),
    )
    wkv, wqo, _ = gathered(attn_piece)
    mine = rolled(layer_in[0])
    rows_in = jnp.concatenate([mine, across(mine)], axis=0)
    inputs = rows_in.astype(F32)
    attn_normed, attn_inverse = norm_parts(inputs)
    attn_act = (attn_normed * attn_gain + attn_shift).astype(BF)
    act_other = core(attn_act)

    zeros_aw = jnp.zeros((aw,), F32)
    q_bias = jnp.concatenate(
        [lax.dynamic_slice_in_dim(query_bias, own_x * aw, aw, 0), zeros_aw]
    )
    v_bias = jnp.concatenate(
        [zeros_aw, lax.dynamic_slice_in_dim(value_bias, own_x * aw, aw, 0)]
    )
    u_bias = lax.dynamic_slice_in_dim(up_bias, own_x * fw, fw, 0)

    query = (mm(attn_act, wqo) + q_bias).astype(BF)
    own_kv = (mm(attn_act, wkv) + v_bias).astype(BF)
    other_kv = (mm(act_other, wkv) + v_bias).astype(BF)

    ff_piece, cot_mine, _, _ = lax.optimization_barrier(
        (by_core(chip_cut(w_up), chip_cut(w_down)), rolled(cotangent[0]), query, own_kv)
    )
    wu, wd, _ = gathered(ff_piece)
    cot = jnp.concatenate([cot_mine, across(cot_mine)], axis=0)
    context, log_total = attention_front(query, own_kv, other_kv, aw)

    def part(a, i):
        return a[i * quarter : (i + 1) * quarter]

    def sent(parts):
        return [move(p) for p, move in zip(parts, (beside, across, corner))]

    def spread(own):
        return jnp.concatenate([own, beside(own), across(own), corner(own)], axis=0)

    def both(own):
        other = beside(own)
        return jnp.where(
            own_y == 0,
            jnp.concatenate([own, other], axis=0),
            jnp.concatenate([other, own], axis=0),
        )

    wu, wd, _ = gathered(ff_piece)
    own_part, *parts = quarters([(context, wqo)])
    parts = sent(parts)
    resid_mid, mlp_own = norm_middle(
        own_part, parts, rows_in[:quarter], out_bias, mlp_gain, mlp_shift
    )
    mlp_act = spread(mlp_own)

    pre_act = mm(mlp_act, wu) + u_bias
    cdf = 0.5 * (1.0 + jax.scipy.special.erf(pre_act * SQRT_HALF))
    hidden = (pre_act * cdf).astype(BF)
    slope = cdf + pre_act * INV_ROOT_TWO_PI * jnp.exp(-0.5 * pre_act * pre_act)
    d_pre = (mm(cot, wd) * slope).astype(BF)
    up_sum = jnp.sum(d_pre.astype(F32), axis=0)[None]
    own_part, *parts = quarters([(d_pre, wu)])
    parts = sent(parts)
    d_mid, d_mid_round, middle_sums = norm_middle_back(
        own_part, parts, resid_mid, cot[:quarter], mlp_gain
    )
    d_mid_all = spread(d_mid_round)

    out_part = mm_nt(after(hidden, d_mid_all), wd)
    out_other = across(out_part[fr:].astype(BF))
    out_part, out_other, _ = lax.optimization_barrier((out_part, out_other, d_mid_all))
    near = out_part[:quarter] + out_other[:quarter].astype(F32) + resid_mid + down_bias
    near = near.astype(BF)
    far = (out_part[quarter:fr] + out_other[quarter:].astype(F32)).astype(BF)
    got = beside(jnp.concatenate([far, near], axis=0)).astype(F32)
    near = (near.astype(F32) + got[:quarter]).astype(BF)
    far = (far.astype(F32) + got[quarter:]).astype(BF)
    layer_out = jnp.where(
        own_y == 0,
        jnp.concatenate([near, far], axis=0),
        jnp.concatenate([far, near], axis=0),
    )

    def shard_sums(first, second):
        keep = by_core(first, second) + core(by_core(second, first).astype(BF)).astype(F32)

        def block(k):
            return lax.dynamic_slice_in_dim(keep, (own_z ^ k) * rows, rows, 0)

        total = block(0)
        sent = [along(block(k).astype(BF), k) for k in range(1, n_dp)]
        for got in sent:
            total = total + got.astype(F32)
        total = total.astype(BF)
        other = across(total)
        left, right = jnp.where(own_x == 0, total, other), jnp.where(own_x == 0, other, total)
        wide = jnp.stack([left, right], axis=0)
        other = core(wide)
        return wide, other

    grad_w_up, grad_w_down = finish(
        *shard_sums(mm_tn(mlp_act, d_pre), mm_tn(cot, hidden)), 1
    )

    d_context = mm(d_mid_all, wqo).astype(BF)
    d_query, kv_own, kv_back, q_sum, v_sum = attention_back(
        query, own_kv, other_kv, context, d_context, log_total, aw
    )
    kv_round = (kv_own + core(kv_back).astype(F32)).astype(BF)
    grad_w_key, grad_w_value, grad_w_query, grad_w_out = finish(
        *shard_sums(
            mm_tn(attn_act, kv_own.astype(BF)) + mm_tn(act_other, kv_back),
            mm_tn(attn_act, d_query) + mm_tn(d_mid_all, context),
        ),
        2,
    )
    own_part, *parts, gain_sum, shift_sum = quarters(
        [(d_query, wqo), (kv_round, wkv)], attn_normed
    )
    parts = sent(parts)
    d_attn_act = own_part
    for p in parts:
        d_attn_act = d_attn_act + p.astype(F32)
    grad_in = d_mid + norm_backward(
        d_attn_act, part(attn_normed, 0), part(attn_inverse, 0), attn_gain
    )
    grad_in = grad_in.astype(BF)
    grad_in = both(grad_in).astype(F32)

    vec = packed(q_sum, v_sum, up_sum, gain_sum, shift_sum, middle_sums)
    k = 1
    while k < n_dp:
        vec = vec + along(vec, k)
        k *= 2
    vec = vec + across(vec)
    vec = vec + core(vec)
    whole = vec[8:]
    whole = whole + beside(whole)
    return (
        layer_out[None],
        grad_in[None],
        grad_w_query,
        grad_w_key,
        grad_w_value,
        grad_w_out,
        grad_w_up,
        grad_w_down,
        vec[2, : 2 * aw],
        vec[2, 2 * aw :],
        whole[0],
        vec[:2].reshape(2 * fw),
        whole[1],
        whole[4],
        whole[5],
        whole[2],
        whole[3],
    )


def solution(mesh):
    square = P("dp", "head")
    acts = P("dp", "seq", None)
    vectors = (P("head"), P("head"), P(), P("head"), P(), P(), P(), P(), P())

    def body(*args):
        return per_device(mesh, *args)

    return jax.shard_map(
        body,
        mesh=mesh,
        in_specs=(acts,) * 2 + (square,) * 6 + vectors,
        out_specs=(acts,) * 2 + (square,) * 6 + vectors,
        check_vma=False,
    )
```

```python
import jax
import jax.numpy as jnp
from jax import lax
from jax.experimental import pallas as pl
from jax.experimental.pallas import tpu as pltpu
from jax.sharding import PartitionSpec as P


HD = 64
NORM_EPS = 1e-05
SQRT_HALF = 0.7071067811865476
INV_ROOT_TWO_PI = 0.3989422804014327
BF = jnp.bfloat16
F32 = jnp.float32


def mm(a, b):
    return jnp.dot(a, b, preferred_element_type=F32)


def mm_nt(a, b):
    return lax.dot_general(a, b, (((1,), (1,)), ((), ())), preferred_element_type=F32)


def mm_tn(a, b):
    return lax.dot_general(a, b, (((0,), (0,)), ((), ())), preferred_element_type=F32)


def norm_parts(values):
    mean_val = jnp.mean(values, axis=-1, keepdims=True)
    centred = values - mean_val
    inverse = lax.rsqrt(jnp.mean(centred * centred, axis=-1, keepdims=True) + NORM_EPS)
    return centred * inverse, inverse


def norm_backward(grad_rows, normed, inverse, gain_vec):
    scaled = grad_rows * gain_vec
    return inverse * (
        scaled
        - jnp.mean(scaled, axis=-1, keepdims=True)
        - normed * jnp.mean(scaled * normed, axis=-1, keepdims=True)
    )


def after(value, *others):
    return lax.optimization_barrier((value, *others))[0]


MIB = 1024 * 1024
VM = pl.BlockSpec(memory_space=pltpu.VMEM)


def assemble(pieces):
    n, (rows, cols) = len(pieces), pieces[0].shape

    def kernel(*refs):
        own = lax.axis_index("dp")
        for k in range(n):
            at = pl.multiple_of(jnp.bitwise_xor(own, k) * rows, rows)
            refs[n][pl.ds(at, rows), :] = refs[k][...]

    return pl.pallas_call(
        kernel,
        out_shape=jax.ShapeDtypeStruct((n * rows, cols), pieces[0].dtype),
        in_specs=[VM] * n,
        out_specs=VM,
        cost_estimate=pl.CostEstimate(
            flops=0, transcendentals=0, bytes_accessed=4 * n * rows * cols
        ),
        compiler_params=pltpu.CompilerParams(vmem_limit_bytes=8 * MIB),
        name="assemble",
    )(*pieces)


def finish(wide, other, count):
    rows, cols = wide.shape[1], wide.shape[2] // count

    def kernel(mine_ref, other_ref, *outs):
        own_c = lax.rem(lax.axis_index("seq"), 2)

        def put(first, second):
            for m, src in enumerate((first, second)):
                for i in range(count):
                    for x in range(2):
                        outs[m * count + i][:, x * cols : (x + 1) * cols] = src[
                            x, :, i * cols : (i + 1) * cols
                        ].astype(F32)

        @pl.when(own_c == 0)
        def _():
            put(mine_ref, other_ref)

        @pl.when(own_c == 1)
        def _():
            put(other_ref, mine_ref)

    return pl.pallas_call(
        kernel,
        out_shape=[jax.ShapeDtypeStruct((rows, 2 * cols), F32)] * (2 * count),
        in_specs=[VM] * 2,
        out_specs=[VM] * (2 * count),
        cost_estimate=pl.CostEstimate(
            flops=0, transcendentals=0, bytes_accessed=24 * rows * cols * count
        ),
        compiler_params=pltpu.CompilerParams(vmem_limit_bytes=8 * MIB),
        name="finish",
    )(wide, other)


def attention_front(query, own_kv, other_kv, width):
    rows = query.shape[0]
    block = rows // 2

    def kernel(q_ref, own_ref, oth_ref, c_ref, lt_ref):
        c_ref[:, :width] = jnp.zeros((rows, width), BF)
        for h in range(width // HD):
            cols = slice(h * HD, (h + 1) * HD)
            late = slice(width + h * HD, width + (h + 1) * HD)
            for at in range(0, rows, block):
                qh = q_ref[at : at + block, cols]
                first = 0.125 * mm_nt(qh, own_ref[:, cols])
                second = 0.125 * mm_nt(qh, oth_ref[:, cols])
                row_max = jnp.maximum(
                    jnp.max(first, axis=-1, keepdims=True), jnp.max(second, axis=-1, keepdims=True)
                )
                first = jnp.exp(first - row_max)
                second = jnp.exp(second - row_max)
                row_sum = jnp.sum(first, axis=-1, keepdims=True) + jnp.sum(
                    second, axis=-1, keepdims=True
                )
                total = mm(first.astype(BF), own_ref[:, late]) + mm(
                    second.astype(BF), oth_ref[:, late]
                )
                c_ref[at : at + block, late] = (total / row_sum).astype(BF)
                lt_ref[at : at + block, h : h + 1] = row_max + jnp.log(row_sum)

    return pl.pallas_call(
        kernel,
        out_shape=[
            jax.ShapeDtypeStruct((rows, 2 * width), BF),
            jax.ShapeDtypeStruct((rows, 128), F32),
        ],
        in_specs=[VM] * 3,
        out_specs=[VM] * 2,
        cost_estimate=pl.CostEstimate(
            flops=8 * rows * rows * width,
            transcendentals=2 * rows * rows * (width // HD),
            bytes_accessed=12 * rows * width,
        ),
        compiler_params=pltpu.CompilerParams(vmem_limit_bytes=24 * MIB),
        name="attention_front",
    )(query, own_kv, other_kv)


def attention_back(query, own_kv, other_kv, context, d_context, log_total, width):
    rows = query.shape[0]

    def kernel(
        q_ref, own_ref, oth_ref, c_ref, dc_ref, lt_ref, dq_ref, down_ref, doth_ref, sum_ref
    ):
        dq_ref[:, width:] = jnp.zeros((rows, width), BF)
        for h in range(width // HD):
            cols = slice(h * HD, (h + 1) * HD)
            late = slice(width + h * HD, width + (h + 1) * HD)
            qh, ch, dch = q_ref[:, cols], c_ref[:, late], dc_ref[:, late]
            delta = jnp.sum(dch.astype(F32) * ch.astype(F32), axis=-1, keepdims=True)
            total = lt_ref[:, h : h + 1]
            d_query = jnp.zeros((rows, HD), F32)
            sums = jnp.zeros((1, HD), F32)
            for src, out in ((own_ref, down_ref), (oth_ref, doth_ref)):
                kh, vh = src[:, cols], src[:, late]
                prob = jnp.exp(0.125 * mm_nt(qh, kh) - total)
                d_score = (0.125 * prob * (mm_nt(dch, vh) - delta)).astype(BF)
                d_query = d_query + mm(d_score, kh)
                out[:, cols] = mm_tn(d_score, qh).astype(out.dtype)
                d_value = mm_tn(prob.astype(BF), dch)
                out[:, late] = d_value.astype(out.dtype)
                sums = sums + jnp.sum(d_value, axis=0, keepdims=True)
            dq_ref[:, cols] = d_query.astype(BF)
            sum_ref[0:1, cols] = jnp.sum(d_query, axis=0, keepdims=True)
            sum_ref[0:1, late] = sums

    return pl.pallas_call(
        kernel,
        out_shape=[
            jax.ShapeDtypeStruct((rows, 2 * width), BF),
            jax.ShapeDtypeStruct((rows, 2 * width), F32),
            jax.ShapeDtypeStruct((rows, 2 * width), BF),
            jax.ShapeDtypeStruct((8, 2 * width), F32),
        ],
        in_specs=[VM] * 6,
        out_specs=[VM] * 4,
        cost_estimate=pl.CostEstimate(
            flops=20 * rows * rows * width,
            transcendentals=2 * rows * rows * (width // HD),
            bytes_accessed=20 * rows * width,
        ),
        compiler_params=pltpu.CompilerParams(vmem_limit_bytes=24 * MIB),
        name="attention_back",
    )(query, own_kv, other_kv, context, d_context, log_total)


def quarters(pairs, normed=None):
    rows, width = pairs[0][0].shape[0], pairs[0][1].shape[0]
    quarter = rows // 4
    n = len(pairs)
    extra = [] if normed is None else [normed]

    def kernel(*refs):
        outs = refs[2 * n + len(extra) :]
        for i in range(4):
            at = slice(i * quarter, (i + 1) * quarter)
            total = mm_nt(refs[0][at, :], refs[1][...])
            for p in range(1, n):
                total = total + mm_nt(refs[2 * p][at, :], refs[2 * p + 1][...])
            outs[i][...] = total.astype(outs[i].dtype)
            if extra:
                gain_sum = jnp.sum(total * refs[2 * n][at, :], axis=0, keepdims=True)
                shift_sum = jnp.sum(total, axis=0, keepdims=True)
                if i == 0:
                    outs[4][...] = gain_sum
                    outs[5][...] = shift_sum
                else:
                    outs[4][...] += gain_sum
                    outs[5][...] += shift_sum

    return pl.pallas_call(
        kernel,
        out_shape=[jax.ShapeDtypeStruct((quarter, width), F32)]
        + [jax.ShapeDtypeStruct((quarter, width), BF)] * 3
        + [jax.ShapeDtypeStruct((1, width), F32)] * (2 * len(extra)),
        in_specs=[VM] * (2 * n + len(extra)),
        out_specs=[VM] * (4 + 2 * len(extra)),
        cost_estimate=pl.CostEstimate(
            flops=2 * n * rows * width * pairs[0][0].shape[1],
            transcendentals=0,
            bytes_accessed=4 * rows * width,
        ),
        compiler_params=pltpu.CompilerParams(vmem_limit_bytes=16 * MIB),
        name="quarters",
    )(*[a for pair in pairs for a in pair], *extra)


def norm_middle(own, others, rows_in, bias, gain, shift):
    def kernel(own_ref, a_ref, b_ref, c_ref, in_ref, bias_ref, gain_ref, shift_ref, mid_ref, act_ref):
        total = own_ref[...] + a_ref[...].astype(F32)
        total = total + b_ref[...].astype(F32) + c_ref[...].astype(F32)
        mid = in_ref[...].astype(F32) + total + bias_ref[...]
        mid_ref[...] = mid
        act_ref[...] = (norm_parts(mid)[0] * gain_ref[...] + shift_ref[...]).astype(BF)

    return pl.pallas_call(
        kernel,
        out_shape=[jax.ShapeDtypeStruct(own.shape, F32), jax.ShapeDtypeStruct(own.shape, BF)],
        in_specs=[VM] * 8,
        out_specs=[VM] * 2,
        cost_estimate=pl.CostEstimate(
            flops=20 * own.size, transcendentals=0, bytes_accessed=18 * own.size
        ),
        compiler_params=pltpu.CompilerParams(vmem_limit_bytes=8 * MIB),
        name="norm_middle",
    )(own, *others, rows_in, bias[None], gain[None], shift[None])


def norm_middle_back(own, others, mid, cotangent, gain):
    def kernel(own_ref, a_ref, b_ref, c_ref, mid_ref, cot_ref, gain_ref, d_ref, dr_ref, sum_ref):
        grad = own_ref[...] + a_ref[...].astype(F32)
        grad = grad + b_ref[...].astype(F32) + c_ref[...].astype(F32)
        normed, inverse = norm_parts(mid_ref[...])
        cot = cot_ref[...].astype(F32)
        d_mid = cot + norm_backward(grad, normed, inverse, gain_ref[...])
        d_ref[...] = d_mid
        dr_ref[...] = d_mid.astype(BF)
        for i, rows in enumerate((d_mid, cot, grad * normed, grad)):
            sum_ref[i : i + 1, :] = jnp.sum(rows, axis=0, keepdims=True)

    return pl.pallas_call(
        kernel,
        out_shape=[
            jax.ShapeDtypeStruct(own.shape, F32),
            jax.ShapeDtypeStruct(own.shape, BF),
            jax.ShapeDtypeStruct((4, own.shape[1]), F32),
        ],
        in_specs=[VM] * 7,
        out_specs=[VM] * 3,
        cost_estimate=pl.CostEstimate(
            flops=30 * own.size, transcendentals=0, bytes_accessed=24 * own.size
        ),
        compiler_params=pltpu.CompilerParams(vmem_limit_bytes=8 * MIB),
        name="norm_middle_back",
    )(own, *others, mid, cotangent, gain[None])


def packed(head_sums, up_sum, gain_sum, shift_sum, middle):
    width, aw = gain_sum.shape[1], head_sums.shape[1] // 2

    def kernel(head_ref, up_ref, gain_ref, shift_ref, mid_ref, out_ref):
        own_x = lax.axis_index("seq") // 2
        out_ref[...] = jnp.zeros((16, width), F32)
        for x in range(2):

            @pl.when(own_x == x)
            def _():
                out_ref[x : x + 1, :] = up_ref[...]
                out_ref[2:3, x * aw : (x + 1) * aw] = head_ref[0:1, :aw]
                out_ref[2:3, (2 + x) * aw : (3 + x) * aw] = head_ref[0:1, aw:]

        out_ref[8:12, :] = mid_ref[...]
        out_ref[12:13, :] = gain_ref[...]
        out_ref[13:14, :] = shift_ref[...]

    return pl.pallas_call(
        kernel,
        out_shape=jax.ShapeDtypeStruct((16, width), F32),
        in_specs=[VM] * 5,
        out_specs=VM,
        cost_estimate=pl.CostEstimate(flops=0, transcendentals=0, bytes_accessed=100 * width),
        compiler_params=pltpu.CompilerParams(vmem_limit_bytes=4 * MIB),
        name="packed",
    )(head_sums, up_sum, gain_sum, shift_sum, middle)


def feed_forward(acts, cotangent, wu, wd, bias):
    quarter, width = acts[0].shape
    rows, hidden = 4 * quarter, wu.shape[1]
    block = 2 * quarter

    def kernel(*refs):
        a_refs, (cot_ref, wu_ref, wd_ref, bias_ref) = refs[:4], refs[4:8]
        act_ref, hid_ref, pre_ref, sum_ref = refs[8:12]
        outs = refs[12:]
        for i in range(4):
            act_ref[i * quarter : (i + 1) * quarter, :] = a_refs[i][...]
        for i in range(2):
            at = slice(i * block, (i + 1) * block)
            pre_act = mm(act_ref[at, :], wu_ref[...]) + bias_ref[...]
            cdf = 0.5 * (1.0 + lax.erf(pre_act * SQRT_HALF))
            hid_ref[at, :] = (pre_act * cdf).astype(BF)
            slope = cdf + pre_act * INV_ROOT_TWO_PI * jnp.exp(-0.5 * pre_act * pre_act)
            d_pre = (mm(cot_ref[at, :], wd_ref[...]) * slope).astype(BF)
            pre_ref[at, :] = d_pre
            total = jnp.sum(d_pre.astype(F32), axis=0, keepdims=True)
            if i == 0:
                sum_ref[...] = total
            else:
                sum_ref[...] += total
            grad = mm_nt(d_pre, wu_ref[...])
            outs[2 * i][...] = grad[:quarter].astype(outs[2 * i].dtype)
            outs[2 * i + 1][...] = grad[quarter:].astype(BF)

    return pl.pallas_call(
        kernel,
        out_shape=[
            jax.ShapeDtypeStruct((rows, width), BF),
            jax.ShapeDtypeStruct((rows, hidden), BF),
            jax.ShapeDtypeStruct((rows, hidden), BF),
            jax.ShapeDtypeStruct((1, hidden), F32),
            jax.ShapeDtypeStruct((quarter, width), F32),
        ]
        + [jax.ShapeDtypeStruct((quarter, width), BF)] * 3,
        in_specs=[VM] * 8,
        out_specs=[VM] * 8,
        cost_estimate=pl.CostEstimate(
            flops=6 * rows * width * hidden,
            transcendentals=2 * rows * hidden,
            bytes_accessed=4 * width * hidden + 10 * rows * width,
        ),
        compiler_params=pltpu.CompilerParams(vmem_limit_bytes=20 * MIB),
        name="feed_forward",
    )(*acts, cotangent, wu, wd, bias[None])


def make_moves(mesh):
    n_dp, n_seq, n_head = mesh.shape["dp"], mesh.shape["seq"], mesh.shape["head"]

    def core(v):
        return lax.ppermute(v, "seq", [(i, i ^ 1) for i in range(n_seq)])

    def across(v):
        return lax.ppermute(v, "seq", [(i, i ^ 2) for i in range(n_seq)])

    def beside(v):
        return lax.ppermute(v, "head", [(i, i ^ 1) for i in range(n_head)])

    def corner(v):
        pairs = [
            (s * n_head + h, (s ^ 2) * n_head + (h ^ 1))
            for s in range(n_seq)
            for h in range(n_head)
        ]
        return lax.ppermute(v, ("seq", "head"), pairs)

    def along(v, k):
        return lax.ppermute(v, "dp", [(i, i ^ k) for i in range(n_dp)])

    return n_dp, core, across, beside, corner, along


def per_device(
    mesh,
    layer_in,
    cotangent,
    w_query,
    w_key,
    w_value,
    w_out,
    w_up,
    w_down,
    query_bias,
    value_bias,
    out_bias,
    up_bias,
    down_bias,
    attn_gain,
    attn_shift,
    mlp_gain,
    mlp_shift,
):
    n_dp, core, across, beside, corner, along = make_moves(mesh)
    own_z = lax.axis_index("dp")
    own_s = lax.axis_index("seq")
    own_y = lax.axis_index("head")
    own_x, own_c = own_s // 2, own_s % 2
    fr, width = layer_in.shape[1], layer_in.shape[2]
    quarter = fr // 2
    rows = width // n_dp
    aw = w_query.shape[1] // 2
    fw = w_up.shape[1] // 2

    def rolled(a):
        return jnp.concatenate(
            [
                lax.dynamic_slice_in_dim(a, own_y * quarter, quarter, 0),
                lax.dynamic_slice_in_dim(a, (1 - own_y) * quarter, quarter, 0),
            ],
            axis=0,
        )

    def chip_cut(w):
        cols = w.shape[1] // 2
        return jnp.where(own_x == 0, w[:, :cols], w[:, cols:])

    def by_core(first, second):
        return jnp.where(own_c == 0, first, second)

    def gathered(piece):
        pieces = [piece] + [along(piece, k) for k in range(1, n_dp)]
        if rows % 16 == 0:
            mine = assemble(pieces)
        else:
            buf = jnp.zeros((n_dp,) + piece.shape, piece.dtype)
            for k, part in enumerate(pieces):
                buf = lax.dynamic_update_slice(buf, part[None], (own_z ^ k, 0, 0))
            mine = buf.reshape(width, piece.shape[1])
        other = core(mine)
        return by_core(mine, other), by_core(other, mine), mine

    attn_piece = by_core(
        jnp.concatenate([chip_cut(w_key), chip_cut(w_value)], axis=1),
        jnp.concatenate([chip_cut(w_query), chip_cut(w_out)], axis=1),
    )
    wkv, wqo, _ = gathered(attn_piece)
    mine = rolled(layer_in[0])
    rows_in = jnp.concatenate([mine, across(mine)], axis=0)
    inputs = rows_in.astype(F32)
    attn_normed, attn_inverse = norm_parts(inputs)
    attn_act = (attn_normed * attn_gain + attn_shift).astype(BF)
    act_other = core(attn_act)

    zeros_aw = jnp.zeros((aw,), F32)
    q_bias = jnp.concatenate(
        [lax.dynamic_slice_in_dim(query_bias, own_x * aw, aw, 0), zeros_aw]
    )
    v_bias = jnp.concatenate(
        [zeros_aw, lax.dynamic_slice_in_dim(value_bias, own_x * aw, aw, 0)]
    )
    u_bias = lax.dynamic_slice_in_dim(up_bias, own_x * fw, fw, 0)

    query = (mm(attn_act, wqo) + q_bias).astype(BF)
    own_kv = (mm(attn_act, wkv) + v_bias).astype(BF)
    other_kv = (mm(act_other, wkv) + v_bias).astype(BF)

    ff_piece = by_core(chip_cut(w_up), chip_cut(w_down))
    ff_piece, _, _ = lax.optimization_barrier((ff_piece, query, own_kv))
    cot_mine = rolled(cotangent[0])
    cot_mine = after(cot_mine, rows_in)
    wu, wd, _ = gathered(ff_piece)
    cot = jnp.concatenate([cot_mine, across(cot_mine)], axis=0)
    context, log_total = attention_front(query, own_kv, other_kv, aw)

    def part(a, i):
        return a[i * quarter : (i + 1) * quarter]

    def sent(parts):
        return [move(p) for p, move in zip(parts, (beside, across, corner))]

    def spread(own):
        return [own, beside(own), across(own), corner(own)]

    def both(own):
        other = beside(own)
        return jnp.where(
            own_y == 0,
            jnp.concatenate([own, other], axis=0),
            jnp.concatenate([other, own], axis=0),
        )

    wu, wd, _ = gathered(ff_piece)
    own_part, *parts = quarters([(context, wqo)])
    parts = sent(parts)
    resid_mid, mlp_own = norm_middle(
        own_part, parts, rows_in[:quarter], out_bias, mlp_gain, mlp_shift
    )
    mlp_acts = spread(mlp_own)
    mlp_act, hidden, d_pre, up_sum, own_part, *parts = feed_forward(
        mlp_acts, cot, wu, wd, u_bias
    )
    parts = sent(parts)
    d_mid, d_mid_round, middle_sums = norm_middle_back(
        own_part, parts, resid_mid, cot[:quarter], mlp_gain
    )
    d_mid_all = jnp.concatenate(spread(d_mid_round), axis=0)

    out_part = mm_nt(hidden, wd)
    out_send = after(out_part[fr:].astype(BF), d_mid_all)
    out_other = across(out_send)
    out_part, out_other, _ = lax.optimization_barrier((out_part, out_other, d_mid_all))
    near = out_part[:quarter] + out_other[:quarter].astype(F32) + resid_mid + down_bias
    near = near.astype(BF)
    far = (out_part[quarter:fr] + out_other[quarter:].astype(F32)).astype(BF)
    got = beside(jnp.concatenate([far, near], axis=0)).astype(F32)
    near = (near.astype(F32) + got[:quarter]).astype(BF)
    far = (far.astype(F32) + got[quarter:]).astype(BF)
    layer_out = jnp.where(
        own_y == 0,
        jnp.concatenate([near, far], axis=0),
        jnp.concatenate([far, near], axis=0),
    )

    def shard_sums(first, second):
        keep = by_core(first, second) + core(by_core(second, first).astype(BF)).astype(F32)

        def block(k):
            return lax.dynamic_slice_in_dim(keep, (own_z ^ k) * rows, rows, 0)

        sent = [along(block(k).astype(BF), k) for k in range(1, n_dp)]
        total = block(0)
        for got in sent:
            total = total + got.astype(F32)
        total = total.astype(BF)
        other = across(total)
        left, right = jnp.where(own_x == 0, total, other), jnp.where(own_x == 0, other, total)
        wide = jnp.stack([left, right], axis=0)
        other = core(wide)
        return wide, other

    grad_w_up, grad_w_down = finish(
        *shard_sums(mm_tn(mlp_act, d_pre), mm_tn(cot, hidden)), 1
    )

    d_context = mm(d_mid_all, wqo).astype(BF)
    d_query, kv_own, kv_back, head_sums = attention_back(
        query, own_kv, other_kv, context, d_context, log_total, aw
    )
    kv_round = (kv_own + core(kv_back).astype(F32)).astype(BF)
    grad_w_key, grad_w_value, grad_w_query, grad_w_out = finish(
        *shard_sums(
            mm_tn(attn_act, kv_own.astype(BF)) + mm_tn(act_other, kv_back),
            mm_tn(attn_act, d_query) + mm_tn(d_mid_all, context),
        ),
        2,
    )
    own_part, *parts, gain_sum, shift_sum = quarters(
        [(d_query, wqo), (kv_round, wkv)], attn_normed
    )
    parts = sent(parts)
    d_attn_act = own_part
    for p in parts:
        d_attn_act = d_attn_act + p.astype(F32)
    grad_in = d_mid + norm_backward(
        d_attn_act, part(attn_normed, 0), part(attn_inverse, 0), attn_gain
    )
    grad_in = grad_in.astype(BF)
    grad_in = both(grad_in).astype(F32)

    vec = packed(head_sums, up_sum, gain_sum, shift_sum, middle_sums)
    k = 1
    while k < n_dp:
        vec = vec + along(vec, k)
        k *= 2
    vec = vec + across(vec)
    vec = vec + core(vec)
    whole = vec[8:]
    whole = whole + beside(whole)
    return (
        layer_out[None],
        grad_in[None],
        grad_w_query,
        grad_w_key,
        grad_w_value,
        grad_w_out,
        grad_w_up,
        grad_w_down,
        vec[2, : 2 * aw],
        vec[2, 2 * aw :],
        whole[0],
        vec[:2].reshape(2 * fw),
        whole[1],
        whole[4],
        whole[5],
        whole[2],
        whole[3],
    )


def solution(mesh):
    square = P("dp", "head")
    acts = P("dp", "seq", None)
    vectors = (P("head"), P("head"), P(), P("head"), P(), P(), P(), P(), P())

    def body(*args):
        return per_device(mesh, *args)

    return jax.shard_map(
        body,
        mesh=mesh,
        in_specs=(acts,) * 2 + (square,) * 6 + vectors,
        out_specs=(acts,) * 2 + (square,) * 6 + vectors,
        check_vma=False,
    )
```

```python
import jax
import jax.numpy as jnp
from jax import lax
from jax.experimental import pallas as pl
from jax.experimental.pallas import tpu as pltpu
from jax.sharding import PartitionSpec as P


HD = 64
NORM_EPS = 1e-05
SQRT_HALF = 0.7071067811865476
INV_ROOT_TWO_PI = 0.3989422804014327
BF = jnp.bfloat16
F32 = jnp.float32


def mm(a, b):
    return jnp.dot(a, b, preferred_element_type=F32)


def mm_nt(a, b):
    return lax.dot_general(a, b, (((1,), (1,)), ((), ())), preferred_element_type=F32)


def mm_tn(a, b):
    return lax.dot_general(a, b, (((0,), (0,)), ((), ())), preferred_element_type=F32)


def norm_parts(values):
    mean_val = jnp.mean(values, axis=-1, keepdims=True)
    centred = values - mean_val
    inverse = lax.rsqrt(jnp.mean(centred * centred, axis=-1, keepdims=True) + NORM_EPS)
    return centred * inverse, inverse


def norm_backward(grad_rows, normed, inverse, gain_vec):
    scaled = grad_rows * gain_vec
    return inverse * (
        scaled
        - jnp.mean(scaled, axis=-1, keepdims=True)
        - normed * jnp.mean(scaled * normed, axis=-1, keepdims=True)
    )


def after(value, *others):
    return lax.optimization_barrier((value, *others))[0]


MIB = 1024 * 1024
VM = pl.BlockSpec(memory_space=pltpu.VMEM)


def assemble(pieces):
    n, (rows, cols) = len(pieces), pieces[0].shape

    def kernel(*refs):
        own = lax.axis_index("dp")
        for k in range(n):
            at = pl.multiple_of(jnp.bitwise_xor(own, k) * rows, rows)
            refs[n][pl.ds(at, rows), :] = refs[k][...]

    return pl.pallas_call(
        kernel,
        out_shape=jax.ShapeDtypeStruct((n * rows, cols), pieces[0].dtype),
        in_specs=[VM] * n,
        out_specs=VM,
        cost_estimate=pl.CostEstimate(
            flops=0, transcendentals=0, bytes_accessed=4 * n * rows * cols
        ),
        compiler_params=pltpu.CompilerParams(vmem_limit_bytes=6 * MIB),
        name="assemble",
    )(*pieces)


def finish(wide, other, count):
    rows, cols = wide.shape[1], wide.shape[2] // count

    def kernel(mine_ref, other_ref, *outs):
        own_c = lax.rem(lax.axis_index("seq"), 2)

        def put(first, second):
            for m, src in enumerate((first, second)):
                for i in range(count):
                    for x in range(2):
                        outs[m * count + i][:, x * cols : (x + 1) * cols] = src[
                            x, :, i * cols : (i + 1) * cols
                        ].astype(F32)

        @pl.when(own_c == 0)
        def _():
            put(mine_ref, other_ref)

        @pl.when(own_c == 1)
        def _():
            put(other_ref, mine_ref)

    return pl.pallas_call(
        kernel,
        out_shape=[jax.ShapeDtypeStruct((rows, 2 * cols), F32)] * (2 * count),
        in_specs=[VM] * 2,
        out_specs=[VM] * (2 * count),
        cost_estimate=pl.CostEstimate(
            flops=0, transcendentals=0, bytes_accessed=24 * rows * cols * count
        ),
        compiler_params=pltpu.CompilerParams(vmem_limit_bytes=8 * MIB),
        name="finish",
    )(wide, other)


def attention_front(query, own_kv, other_kv, width):
    rows = query.shape[0]
    block = rows // 2

    def kernel(q_ref, own_ref, oth_ref, c_ref, lt_ref):
        c_ref[:, :width] = jnp.zeros((rows, width), BF)
        for h in range(width // HD):
            cols = slice(h * HD, (h + 1) * HD)
            late = slice(width + h * HD, width + (h + 1) * HD)
            for at in range(0, rows, block):
                qh = q_ref[at : at + block, cols]
                first = 0.125 * mm_nt(qh, own_ref[:, cols])
                second = 0.125 * mm_nt(qh, oth_ref[:, cols])
                row_max = jnp.maximum(
                    jnp.max(first, axis=-1, keepdims=True), jnp.max(second, axis=-1, keepdims=True)
                )
                first = jnp.exp(first - row_max)
                second = jnp.exp(second - row_max)
                row_sum = jnp.sum(first, axis=-1, keepdims=True) + jnp.sum(
                    second, axis=-1, keepdims=True
                )
                total = mm(first.astype(BF), own_ref[:, late]) + mm(
                    second.astype(BF), oth_ref[:, late]
                )
                c_ref[at : at + block, late] = (total / row_sum).astype(BF)
                lt_ref[at : at + block, h : h + 1] = row_max + jnp.log(row_sum)

    return pl.pallas_call(
        kernel,
        out_shape=[
            jax.ShapeDtypeStruct((rows, 2 * width), BF),
            jax.ShapeDtypeStruct((rows, 128), F32),
        ],
        in_specs=[VM] * 3,
        out_specs=[VM] * 2,
        cost_estimate=pl.CostEstimate(
            flops=8 * rows * rows * width,
            transcendentals=2 * rows * rows * (width // HD),
            bytes_accessed=12 * rows * width,
        ),
        compiler_params=pltpu.CompilerParams(vmem_limit_bytes=14 * MIB),
        name="attention_front",
    )(query, own_kv, other_kv)


def attention_back(query, own_kv, other_kv, context, d_context, log_total, width):
    rows = query.shape[0]

    def kernel(
        q_ref, own_ref, oth_ref, c_ref, dc_ref, lt_ref, dq_ref, down_ref, doth_ref, sum_ref
    ):
        dq_ref[:, width:] = jnp.zeros((rows, width), BF)
        for h in range(width // HD):
            cols = slice(h * HD, (h + 1) * HD)
            late = slice(width + h * HD, width + (h + 1) * HD)
            qh, ch, dch = q_ref[:, cols], c_ref[:, late], dc_ref[:, late]
            delta = jnp.sum(dch.astype(F32) * ch.astype(F32), axis=-1, keepdims=True)
            total = lt_ref[:, h : h + 1]
            d_query = jnp.zeros((rows, HD), F32)
            sums = jnp.zeros((1, HD), F32)
            for src, out in ((own_ref, down_ref), (oth_ref, doth_ref)):
                kh, vh = src[:, cols], src[:, late]
                prob = jnp.exp(0.125 * mm_nt(qh, kh) - total)
                d_score = (0.125 * prob * (mm_nt(dch, vh) - delta)).astype(BF)
                d_query = d_query + mm(d_score, kh)
                out[:, cols] = mm_tn(d_score, qh).astype(out.dtype)
                d_value = mm_tn(prob.astype(BF), dch)
                out[:, late] = d_value.astype(out.dtype)
                sums = sums + jnp.sum(d_value, axis=0, keepdims=True)
            dq_ref[:, cols] = d_query.astype(BF)
            sum_ref[0:1, cols] = jnp.sum(d_query, axis=0, keepdims=True)
            sum_ref[0:1, late] = sums

    return pl.pallas_call(
        kernel,
        out_shape=[
            jax.ShapeDtypeStruct((rows, 2 * width), BF),
            jax.ShapeDtypeStruct((rows, 2 * width), F32),
            jax.ShapeDtypeStruct((rows, 2 * width), BF),
            jax.ShapeDtypeStruct((8, 2 * width), F32),
        ],
        in_specs=[VM] * 6,
        out_specs=[VM] * 4,
        cost_estimate=pl.CostEstimate(
            flops=20 * rows * rows * width,
            transcendentals=2 * rows * rows * (width // HD),
            bytes_accessed=20 * rows * width,
        ),
        compiler_params=pltpu.CompilerParams(vmem_limit_bytes=16 * MIB),
        name="attention_back",
    )(query, own_kv, other_kv, context, d_context, log_total)


def quarters(pairs, normed=None):
    rows, width = pairs[0][0].shape[0], pairs[0][1].shape[0]
    quarter = rows // 4
    n = len(pairs)
    extra = [] if normed is None else [normed]

    def kernel(*refs):
        outs = refs[2 * n + len(extra) :]
        for i in range(4):
            at = slice(i * quarter, (i + 1) * quarter)
            total = mm_nt(refs[0][at, :], refs[1][...])
            for p in range(1, n):
                total = total + mm_nt(refs[2 * p][at, :], refs[2 * p + 1][...])
            outs[i][...] = total.astype(outs[i].dtype)
            if extra:
                gain_sum = jnp.sum(total * refs[2 * n][at, :], axis=0, keepdims=True)
                shift_sum = jnp.sum(total, axis=0, keepdims=True)
                if i == 0:
                    outs[4][...] = gain_sum
                    outs[5][...] = shift_sum
                else:
                    outs[4][...] += gain_sum
                    outs[5][...] += shift_sum

    return pl.pallas_call(
        kernel,
        out_shape=[jax.ShapeDtypeStruct((quarter, width), F32)]
        + [jax.ShapeDtypeStruct((quarter, width), BF)] * 3
        + [jax.ShapeDtypeStruct((1, width), F32)] * (2 * len(extra)),
        in_specs=[VM] * (2 * n + len(extra)),
        out_specs=[VM] * (4 + 2 * len(extra)),
        cost_estimate=pl.CostEstimate(
            flops=2 * n * rows * width * pairs[0][0].shape[1],
            transcendentals=0,
            bytes_accessed=4 * rows * width,
        ),
        compiler_params=pltpu.CompilerParams(vmem_limit_bytes=12 * MIB),
        name="quarters",
    )(*[a for pair in pairs for a in pair], *extra)


def norm_middle(own, others, rows_in, bias, gain, shift):
    def kernel(own_ref, a_ref, b_ref, c_ref, in_ref, bias_ref, gain_ref, shift_ref, mid_ref, act_ref):
        total = own_ref[...] + a_ref[...].astype(F32)
        total = total + b_ref[...].astype(F32) + c_ref[...].astype(F32)
        mid = in_ref[...].astype(F32) + total + bias_ref[...]
        mid_ref[...] = mid
        act_ref[...] = (norm_parts(mid)[0] * gain_ref[...] + shift_ref[...]).astype(BF)

    return pl.pallas_call(
        kernel,
        out_shape=[jax.ShapeDtypeStruct(own.shape, F32), jax.ShapeDtypeStruct(own.shape, BF)],
        in_specs=[VM] * 8,
        out_specs=[VM] * 2,
        cost_estimate=pl.CostEstimate(
            flops=20 * own.size, transcendentals=0, bytes_accessed=18 * own.size
        ),
        compiler_params=pltpu.CompilerParams(vmem_limit_bytes=4 * MIB),
        name="norm_middle",
    )(own, *others, rows_in, bias[None], gain[None], shift[None])


def norm_middle_back(own, others, mid, cotangent, gain):
    def kernel(own_ref, a_ref, b_ref, c_ref, mid_ref, cot_ref, gain_ref, d_ref, dr_ref, sum_ref):
        grad = own_ref[...] + a_ref[...].astype(F32)
        grad = grad + b_ref[...].astype(F32) + c_ref[...].astype(F32)
        normed, inverse = norm_parts(mid_ref[...])
        cot = cot_ref[...].astype(F32)
        d_mid = cot + norm_backward(grad, normed, inverse, gain_ref[...])
        d_ref[...] = d_mid
        dr_ref[...] = d_mid.astype(BF)
        for i, rows in enumerate((d_mid, cot, grad * normed, grad)):
            sum_ref[i : i + 1, :] = jnp.sum(rows, axis=0, keepdims=True)

    return pl.pallas_call(
        kernel,
        out_shape=[
            jax.ShapeDtypeStruct(own.shape, F32),
            jax.ShapeDtypeStruct(own.shape, BF),
            jax.ShapeDtypeStruct((4, own.shape[1]), F32),
        ],
        in_specs=[VM] * 7,
        out_specs=[VM] * 3,
        cost_estimate=pl.CostEstimate(
            flops=30 * own.size, transcendentals=0, bytes_accessed=24 * own.size
        ),
        compiler_params=pltpu.CompilerParams(vmem_limit_bytes=5 * MIB),
        name="norm_middle_back",
    )(own, *others, mid, cotangent, gain[None])


def packed(head_sums, up_sum, gain_sum, shift_sum, middle):
    width, aw = gain_sum.shape[1], head_sums.shape[1] // 2

    def kernel(head_ref, up_ref, gain_ref, shift_ref, mid_ref, out_ref):
        own_x = lax.axis_index("seq") // 2
        out_ref[...] = jnp.zeros((16, width), F32)
        for x in range(2):

            @pl.when(own_x == x)
            def _():
                out_ref[x : x + 1, :] = up_ref[...]
                out_ref[2:3, x * aw : (x + 1) * aw] = head_ref[0:1, :aw]
                out_ref[2:3, (2 + x) * aw : (3 + x) * aw] = head_ref[0:1, aw:]

        out_ref[8:12, :] = mid_ref[...]
        out_ref[12:13, :] = gain_ref[...]
        out_ref[13:14, :] = shift_ref[...]

    return pl.pallas_call(
        kernel,
        out_shape=jax.ShapeDtypeStruct((16, width), F32),
        in_specs=[VM] * 5,
        out_specs=VM,
        cost_estimate=pl.CostEstimate(flops=0, transcendentals=0, bytes_accessed=100 * width),
        compiler_params=pltpu.CompilerParams(vmem_limit_bytes=4 * MIB),
        name="packed",
    )(head_sums, up_sum, gain_sum, shift_sum, middle)


def feed_forward(acts, cotangent, wu, wd, bias):
    quarter, width = acts[0].shape
    rows, hidden = 4 * quarter, wu.shape[1]
    block = 2 * quarter

    def kernel(*refs):
        a_refs, (cot_ref, wu_ref, wd_ref, bias_ref) = refs[:4], refs[4:8]
        act_ref, hid_ref, pre_ref, sum_ref = refs[8:12]
        outs = refs[12:]
        for i in range(4):
            act_ref[i * quarter : (i + 1) * quarter, :] = a_refs[i][...]
        for i in range(2):
            at = slice(i * block, (i + 1) * block)
            pre_act = mm(act_ref[at, :], wu_ref[...]) + bias_ref[...]
            cdf = 0.5 * (1.0 + lax.erf(pre_act * SQRT_HALF))
            hid_ref[at, :] = (pre_act * cdf).astype(BF)
            slope = cdf + pre_act * INV_ROOT_TWO_PI * jnp.exp(-0.5 * pre_act * pre_act)
            d_pre = (mm(cot_ref[at, :], wd_ref[...]) * slope).astype(BF)
            pre_ref[at, :] = d_pre
            total = jnp.sum(d_pre.astype(F32), axis=0, keepdims=True)
            if i == 0:
                sum_ref[...] = total
            else:
                sum_ref[...] += total
            grad = mm_nt(d_pre, wu_ref[...])
            outs[2 * i][...] = grad[:quarter].astype(outs[2 * i].dtype)
            outs[2 * i + 1][...] = grad[quarter:].astype(BF)

    return pl.pallas_call(
        kernel,
        out_shape=[
            jax.ShapeDtypeStruct((rows, width), BF),
            jax.ShapeDtypeStruct((rows, hidden), BF),
            jax.ShapeDtypeStruct((rows, hidden), BF),
            jax.ShapeDtypeStruct((1, hidden), F32),
            jax.ShapeDtypeStruct((quarter, width), F32),
        ]
        + [jax.ShapeDtypeStruct((quarter, width), BF)] * 3,
        in_specs=[VM] * 8,
        out_specs=[VM] * 8,
        cost_estimate=pl.CostEstimate(
            flops=6 * rows * width * hidden,
            transcendentals=2 * rows * hidden,
            bytes_accessed=4 * width * hidden + 10 * rows * width,
        ),
        compiler_params=pltpu.CompilerParams(vmem_limit_bytes=16 * MIB),
        name="feed_forward",
    )(*acts, cotangent, wu, wd, bias[None])


def make_moves(mesh):
    n_dp, n_seq, n_head = mesh.shape["dp"], mesh.shape["seq"], mesh.shape["head"]

    def core(v):
        return lax.ppermute(v, "seq", [(i, i ^ 1) for i in range(n_seq)])

    def across(v):
        return lax.ppermute(v, "seq", [(i, i ^ 2) for i in range(n_seq)])

    def beside(v):
        return lax.ppermute(v, "head", [(i, i ^ 1) for i in range(n_head)])

    def corner(v):
        pairs = [
            (s * n_head + h, (s ^ 2) * n_head + (h ^ 1))
            for s in range(n_seq)
            for h in range(n_head)
        ]
        return lax.ppermute(v, ("seq", "head"), pairs)

    def along(v, k):
        return lax.ppermute(v, "dp", [(i, i ^ k) for i in range(n_dp)])

    return n_dp, core, across, beside, corner, along


def per_device(
    mesh,
    layer_in,
    cotangent,
    w_query,
    w_key,
    w_value,
    w_out,
    w_up,
    w_down,
    query_bias,
    value_bias,
    out_bias,
    up_bias,
    down_bias,
    attn_gain,
    attn_shift,
    mlp_gain,
    mlp_shift,
):
    n_dp, core, across, beside, corner, along = make_moves(mesh)
    own_z = lax.axis_index("dp")
    own_s = lax.axis_index("seq")
    own_y = lax.axis_index("head")
    own_x, own_c = own_s // 2, own_s % 2
    fr, width = layer_in.shape[1], layer_in.shape[2]
    quarter = fr // 2
    rows = width // n_dp
    aw = w_query.shape[1] // 2
    fw = w_up.shape[1] // 2

    def rolled(a):
        return jnp.concatenate(
            [
                lax.dynamic_slice_in_dim(a, own_y * quarter, quarter, 0),
                lax.dynamic_slice_in_dim(a, (1 - own_y) * quarter, quarter, 0),
            ],
            axis=0,
        )

    def chip_cut(w):
        cols = w.shape[1] // 2
        return jnp.where(own_x == 0, w[:, :cols], w[:, cols:])

    def by_core(first, second):
        return jnp.where(own_c == 0, first, second)

    def gathered(piece):
        pieces = [piece] + [along(piece, k) for k in range(1, n_dp)]
        if rows % 16 == 0:
            mine = assemble(pieces)
        else:
            buf = jnp.zeros((n_dp,) + piece.shape, piece.dtype)
            for k, part in enumerate(pieces):
                buf = lax.dynamic_update_slice(buf, part[None], (own_z ^ k, 0, 0))
            mine = buf.reshape(width, piece.shape[1])
        other = core(mine)
        return by_core(mine, other), by_core(other, mine), mine

    attn_piece = by_core(
        jnp.concatenate([chip_cut(w_key), chip_cut(w_value)], axis=1),
        jnp.concatenate([chip_cut(w_query), chip_cut(w_out)], axis=1),
    )
    wkv, wqo, _ = gathered(attn_piece)
    mine = rolled(layer_in[0])
    rows_in = jnp.concatenate([mine, across(mine)], axis=0)
    inputs = rows_in.astype(F32)
    attn_normed, attn_inverse = norm_parts(inputs)
    attn_act = (attn_normed * attn_gain + attn_shift).astype(BF)
    act_other = core(attn_act)

    zeros_aw = jnp.zeros((aw,), F32)
    q_bias = jnp.concatenate(
        [lax.dynamic_slice_in_dim(query_bias, own_x * aw, aw, 0), zeros_aw]
    )
    v_bias = jnp.concatenate(
        [zeros_aw, lax.dynamic_slice_in_dim(value_bias, own_x * aw, aw, 0)]
    )
    u_bias = lax.dynamic_slice_in_dim(up_bias, own_x * fw, fw, 0)

    query = (mm(attn_act, wqo) + q_bias).astype(BF)
    own_kv = (mm(attn_act, wkv) + v_bias).astype(BF)
    other_kv = (mm(act_other, wkv) + v_bias).astype(BF)

    ff_piece = by_core(chip_cut(w_up), chip_cut(w_down))
    ff_piece, _, _ = lax.optimization_barrier((ff_piece, query, own_kv))
    cot_mine = rolled(cotangent[0])
    cot_mine = after(cot_mine, rows_in)
    wu, wd, _ = gathered(ff_piece)
    cot = jnp.concatenate([cot_mine, across(cot_mine)], axis=0)
    context, log_total = attention_front(query, own_kv, other_kv, aw)

    def part(a, i):
        return a[i * quarter : (i + 1) * quarter]

    def sent(parts):
        return [move(p) for p, move in zip(parts, (beside, across, corner))]

    def spread(own):
        return [own, beside(own), across(own), corner(own)]

    def both(own):
        other = beside(own)
        return jnp.where(
            own_y == 0,
            jnp.concatenate([own, other], axis=0),
            jnp.concatenate([other, own], axis=0),
        )

    wu, wd, _ = gathered(ff_piece)
    own_part, *parts = quarters([(context, wqo)])
    parts = sent(parts)
    resid_mid, mlp_own = norm_middle(
        own_part, parts, rows_in[:quarter], out_bias, mlp_gain, mlp_shift
    )
    mlp_acts = spread(mlp_own)
    mlp_act, hidden, d_pre, up_sum, own_part, *parts = feed_forward(
        mlp_acts, cot, wu, wd, u_bias
    )
    parts = sent(parts)
    d_mid, d_mid_round, middle_sums = norm_middle_back(
        own_part, parts, resid_mid, cot[:quarter], mlp_gain
    )
    d_mid_all = jnp.concatenate(spread(d_mid_round), axis=0)

    out_part = mm_nt(hidden, wd)
    out_send = after(out_part[fr:].astype(BF), d_mid_all)
    out_other = across(out_send)
    out_part, out_other, _ = lax.optimization_barrier((out_part, out_other, d_mid_all))
    near = out_part[:quarter] + out_other[:quarter].astype(F32) + resid_mid + down_bias
    near = near.astype(BF)
    far = (out_part[quarter:fr] + out_other[quarter:].astype(F32)).astype(BF)
    got = beside(jnp.concatenate([far, near], axis=0)).astype(F32)
    near = (near.astype(F32) + got[:quarter]).astype(BF)
    far = (far.astype(F32) + got[quarter:]).astype(BF)
    layer_out = jnp.where(
        own_y == 0,
        jnp.concatenate([near, far], axis=0),
        jnp.concatenate([far, near], axis=0),
    )

    def shard_sums(first, second):
        keep = by_core(first, second) + core(by_core(second, first).astype(BF)).astype(F32)

        def block(k):
            return lax.dynamic_slice_in_dim(keep, (own_z ^ k) * rows, rows, 0)

        sent = [along(block(k).astype(BF), k) for k in range(1, n_dp)]
        total = block(0)
        for got in sent:
            total = total + got.astype(F32)
        total = total.astype(BF)
        other = across(total)
        left, right = jnp.where(own_x == 0, total, other), jnp.where(own_x == 0, other, total)
        wide = jnp.stack([left, right], axis=0)
        other = core(wide)
        return wide, other

    grad_w_up, grad_w_down = finish(
        *shard_sums(mm_tn(mlp_act, d_pre), mm_tn(cot, hidden)), 1
    )

    d_context = mm(d_mid_all, wqo).astype(BF)
    d_query, kv_own, kv_back, head_sums = attention_back(
        query, own_kv, other_kv, context, d_context, log_total, aw
    )
    kv_round = (kv_own + core(kv_back).astype(F32)).astype(BF)
    grad_w_key, grad_w_value, grad_w_query, grad_w_out = finish(
        *shard_sums(
            mm_tn(attn_act, kv_own.astype(BF)) + mm_tn(act_other, kv_back),
            mm_tn(attn_act, d_query) + mm_tn(d_mid_all, context),
        ),
        2,
    )
    own_part, *parts, gain_sum, shift_sum = quarters(
        [(d_query, wqo), (kv_round, wkv)], attn_normed
    )
    parts = sent(parts)
    d_attn_act = own_part
    for p in parts:
        d_attn_act = d_attn_act + p.astype(F32)
    grad_in = d_mid + norm_backward(
        d_attn_act, part(attn_normed, 0), part(attn_inverse, 0), attn_gain
    )
    grad_in = grad_in.astype(BF)
    grad_in = both(grad_in).astype(F32)

    vec = packed(head_sums, up_sum, gain_sum, shift_sum, middle_sums)
    k = 1
    while k < n_dp:
        vec = vec + along(vec, k)
        k *= 2
    vec = vec + across(vec)
    vec = vec + core(vec)
    whole = vec[8:]
    whole = whole + beside(whole)
    return (
        layer_out[None],
        grad_in[None],
        grad_w_query,
        grad_w_key,
        grad_w_value,
        grad_w_out,
        grad_w_up,
        grad_w_down,
        vec[2, : 2 * aw],
        vec[2, 2 * aw :],
        whole[0],
        vec[:2].reshape(2 * fw),
        whole[1],
        whole[4],
        whole[5],
        whole[2],
        whole[3],
    )


def solution(mesh):
    square = P("dp", "head")
    acts = P("dp", "seq", None)
    vectors = (P("head"), P("head"), P(), P("head"), P(), P(), P(), P(), P())

    def body(*args):
        return per_device(mesh, *args)

    return jax.shard_map(
        body,
        mesh=mesh,
        in_specs=(acts,) * 2 + (square,) * 6 + vectors,
        out_specs=(acts,) * 2 + (square,) * 6 + vectors,
        check_vma=False,
    )
```
